128 devices in a mesh: lon: 8 (over x, core), lat: 16 (over y, z).
Axes of the slice: x: 4, y: 4, z: 4, core: 2. Of those that a mesh axis runs over, the one named last changes fastest.
Arguments:
- ocean_status: float32 [128, 3, 128, 4096], P(None, None, 'lat', 'lon'), may hold values from -4 to 4
- height_driver: bfloat16 [128, 128, 4096], P(None, 'lat', 'lon'), may hold values from -4 to 4
- obs_index: int32 [16, 8, 64], P('lat', 'lon'), may hold values from 0 to 4095
- obs_value: float32 [16, 8, 64], P('lat', 'lon'), may hold values from -5 to 5
- obs_error: float32 [16, 8, 64], P('lat', 'lon'), may hold values from 1 to 10
Outputs:
- analysis: float32 [128, 3, 128, 4096], P(None, None, 'lat', 'lon')
The draws below stay inside these ranges and needn't reach their ends.
Inputs may be any that keep to these rules, and one draw needn't show every extreme that they name: `obs_index`: an observation's cell inside its device's tile, the tile's row times 512 plus its column.
All inputs are finite; a program needn't handle non-finite values.
Results may differ from the reference program's by a relative error of at most 0.0003.
Values sent between devices are 32-bit elements; how exact they have to be, the bound alone decides.
No kernel may reach another device: no remote copies, remote signals or barrier semaphores. Data moves between devices by JAX's collectives and lax.ppermute only.
A program may use at most 128 MiB of HBM per device.

```python
import math
import jax
import jax.numpy as jnp
from jax import lax

MEMBERS = 128
CLAT = 8
CLON = 512
OBS_DEV = 64
NS_ITERS = 14
NLAT = 128
NLON = 4096
N_LON = 8
N_LAT = 16


def touch_ends(array, stream_key, least, high):
    longest = array.shape.index(max(array.shape))
    spots = []
    for shift in (0, 1):
        where = [jax.random.randint(jax.random.fold_in(stream_key, axis), (), 0, length) for axis, length in enumerate(array.shape)]
        where[longest] = (where[longest] + shift) % array.shape[longest]
        spots.append(tuple(where))
    return array.at[spots[0]].set(least).at[spots[1]].set(high)


def shard_levels(rng, extent, pieces, least, largest):
    level = 1.0
    for position, parts in pieces:
        steps = jax.random.uniform(jax.random.fold_in(jax.random.fold_in(rng, 6), position), (parts,), jnp.float32, least / len(pieces), largest / len(pieces))
        level = level * jnp.repeat(jnp.exp(steps), extent[position] // parts).reshape((-1,) + (1,) * (len(extent) - 1 - position))
    return level


def noise(rng, dims, scale, most, split=(), kind=jnp.bfloat16):
    loudness = shard_levels(rng, dims, split, -0.22, 0.18) if split else 1.0
    entries = jax.random.normal(rng, dims, jnp.float32) * scale * loudness
    return jnp.minimum(jnp.maximum(entries, -most), most).astype(kind)


def setup_inputs(seed: int = 0) -> dict:
    key_list = jax.random.split(jax.random.key(seed), 6)
    ocean_status = noise(key_list[0], (MEMBERS, 3, NLAT, NLON), 1.0, 4.0, ((2, 16), (3, 8)), jnp.float32)
    height_driver = noise(key_list[1], (MEMBERS, NLAT, NLON), 1.0, 4.0, ((1, 16), (2, 8)))
    obs_index = touch_ends(jax.random.randint(key_list[2], (N_LAT, N_LON, OBS_DEV), 0, CLAT * CLON), jax.random.fold_in(key_list[2], 1), 0, (CLAT * CLON) - 1).astype(jnp.int32)
    obs_value = noise(key_list[3], (N_LAT, N_LON, OBS_DEV), 1.0, 5.0, ((0, 16), (1, 8)), jnp.float32)
    obs_error = jnp.clip(jnp.exp(math.log(10.0) - 2.3025851 * jax.random.uniform(key_list[4], (N_LAT, N_LON, OBS_DEV), jnp.float32) ** shard_levels(key_list[4], (N_LAT, N_LON, OBS_DEV), ((0, 16), (1, 8)), -0.2, 0.2)), 1.0, 10.0)
    return {"ocean_status": ocean_status, "height_driver": height_driver, "obs_index": obs_index, "obs_value": obs_value, "obs_error": obs_error}


PRECISE = lax.Precision.HIGHEST
GRAVITY = 1.0
DEPTH_MEAN = 1.0
COURANT = 0.2
DIFFUSION = 0.1
FORCE_STEP = 0.5
CORIOLIS_MAX = 0.3

def centre(field):
    return field[..., 1:-1, 1:-1]

def east_of(field):
    return field[..., 1:-1, 2:]

def west_of(field):
    return field[..., 1:-1, :-2]

def north_of(field):
    return field[..., 2:, 1:-1]

def south_of(field):
    return field[..., :-2, 1:-1]

def along_x(field):
    return 0.5 * (east_of(field) - west_of(field))

def along_y(field):
    return 0.5 * (north_of(field) - south_of(field))

def laplace(field):
    return east_of(field) + west_of(field) + north_of(field) + south_of(field) - 4.0 * centre(field)

def advance(padded, pushes, coriolis):
    height = padded[..., 0, :, :]
    zonal = padded[..., 1, :, :]
    merid = padded[..., 2, :, :]
    height_c = centre(height)
    zonal_c = centre(zonal)
    merid_c = centre(merid)
    flux_x = (DEPTH_MEAN + height) * zonal
    flux_y = (DEPTH_MEAN + height) * merid
    height_new = height_c - COURANT * (along_x(flux_x) + along_y(flux_y)) + DIFFUSION * laplace(height) + FORCE_STEP * pushes
    zonal_new = zonal_c - COURANT * (GRAVITY * along_x(height) + zonal_c * along_x(zonal) + merid_c * along_y(zonal)) + COURANT * coriolis * merid_c + DIFFUSION * laplace(zonal)
    merid_new = merid_c - COURANT * (GRAVITY * along_y(height) + zonal_c * along_x(merid) + merid_c * along_y(merid)) - COURANT * coriolis * zonal_c + DIFFUSION * laplace(merid)
    return jnp.stack([height_new, zonal_new, merid_new], axis=-3)

def pad_grid(fields):
    rows = jnp.pad(fields, [(0, 0)] * (fields.ndim - 2) + [(1, 1), (0, 0)])
    return jnp.concatenate([rows[..., -1:], rows, rows[..., :1]], axis=-1)

def coriolis_rows(start, count, total):
    rows = start + jnp.arange(count, dtype=jnp.float32)
    return (CORIOLIS_MAX * (2.0 * (rows + 0.5) / total - 1.0))[:, None]

def ensemble_weights(gram, innovation_sum, members):
    identity = jnp.eye(members, dtype=jnp.float32)
    amat = (members - 1) * identity + gram
    scale = jnp.sqrt(jnp.sum(amat * amat))
    upper = amat / scale
    lower = identity
    for repeat in range(NS_ITERS):
        factor = 1.5 * identity - 0.5 * jnp.dot(lower, upper, precision=PRECISE)
        upper = jnp.dot(upper, factor, precision=PRECISE)
        lower = jnp.dot(factor, lower, precision=PRECISE)
    root = lower / jnp.sqrt(scale)
    inverse = jnp.dot(root, root, precision=PRECISE)
    mean_shift = jnp.dot(inverse, innovation_sum, precision=PRECISE)
    return math.sqrt(members - 1) * root + mean_shift[:, None]

def observe_sums(measurement_readings, values, errors):
    obs_mean = lax.optimization_barrier(jnp.mean(measurement_readings, axis=0))
    obs_spread = measurement_readings - obs_mean
    innovation = values - obs_mean
    inv_error = 1.0 / errors
    gram = jnp.dot(obs_spread * inv_error, obs_spread.T, precision=PRECISE)
    innovation_sum = jnp.dot(obs_spread, inv_error * innovation, precision=PRECISE)
    return (gram, innovation_sum)

def ensemble_mapping_operator(ensemble, blending_coefficients):
    ens_mean = lax.optimization_barrier(jnp.mean(ensemble, axis=0, keepdims=True))
    spread = ensemble - ens_mean
    return ens_mean + jnp.einsum('kfyx,km->mfyx', spread, blending_coefficients, precision=PRECISE)

def reference(ocean_status, height_driver, obs_index, obs_value, obs_error):
    coriolis = coriolis_rows(0.0, NLAT, NLAT)

    def single_run_projection(member_pair):
        fields, pushes = member_pair
        pushes = pushes.astype(jnp.float32)
        for repeat in range(2):
            fields = advance(pad_grid(fields), pushes, coriolis)
        return fields
    projected_ensemble_states = lax.map(single_run_projection, (ocean_status, height_driver))
    block_north_extent = jnp.arange(N_LAT, dtype=jnp.int32)[:, None, None] * CLAT + obs_index // CLON
    block_east_extent = jnp.arange(N_LON, dtype=jnp.int32)[None, :, None] * CLON + obs_index % CLON
    measurement_readings = projected_ensemble_states[:, 0, block_north_extent.reshape(-1), block_east_extent.reshape(-1)]
    gram, innovation_sum = observe_sums(measurement_readings, obs_value.reshape(-1), obs_error.reshape(-1))
    blending_coefficients = ensemble_weights(gram, innovation_sum, MEMBERS)
    return ensemble_mapping_operator(projected_ensemble_states, blending_coefficients)
```

```python
import functools
import math

import jax
import jax.numpy as jnp
from jax import lax
from jax.experimental import pallas as pl
from jax.experimental.pallas import tpu as pltpu
from jax.sharding import PartitionSpec as P

NS_ITERS = 14
PRECISE = lax.Precision.HIGHEST
CORIOLIS_MAX = 0.3
F32 = jnp.float32
BF16 = jnp.bfloat16

VMEM = pl.BlockSpec(memory_space=pltpu.VMEM)
SMEM = pl.BlockSpec(memory_space=pltpu.SMEM)
ANY = pl.BlockSpec(memory_space=pl.ANY)


def shape(*dims, dtype=F32):
    return jax.ShapeDtypeStruct(dims, dtype)


def call(body, name, outs, ins, out_specs, scratch=(), **extra):
    return pl.pallas_call(
        body,
        name=name,
        out_shape=outs,
        in_specs=ins,
        out_specs=out_specs,
        scratch_shapes=scratch,
        compiler_params=pltpu.CompilerParams(vmem_limit_bytes=60000 * 1024),
        **extra,
    )


def edge_body(state, south, north, sems):
    members = state.shape[0]
    rows = state.shape[2]
    parts = 4
    step = members // parts
    copies = []
    for row, out in ((0, south), (rows - 1, north)):
        for f in range(3):
            for p in range(parts):
                span = pl.ds(p * step, step)
                copies.append(
                    pltpu.make_async_copy(state.at[span, f, row, :], out.at[f, span, :], sems.at[len(copies)])
                )
    for c in copies:
        c.start()
    for c in copies:
        c.wait()


def put_columns(load, rows, g, west_out, east_out, keep):
    lane = lax.broadcasted_iota(jnp.int32, (8, 128), 1)
    west = jnp.zeros((8, 128), F32) if keep is None else keep[0]
    east = jnp.zeros((8, 128), F32) if keep is None else keep[1]
    for f in range(3):
        for r in rows:
            at = 8 * f + r
            west = jnp.where(lane == at, pltpu.roll(load(f, r, g, 0), at, 1), west)
            east = jnp.where(lane == at, pltpu.roll(load(f, r, g, 3), (at + 1) % 128, 1), east)
    west_out[pl.ds(g * 8, 8), :] = west
    east_out[pl.ds(g * 8, 8), :] = east


def row_loader(inner, south, north, below=None, above=None):
    def load(f, r, g, c):
        span, lanes = pl.ds(g * 8, 8), pl.ds(c * 128, 128)
        if r == -1:
            return below[f, span, lanes]
        if r == 0:
            return south[f, span, lanes]
        if r == 7:
            return north[f, span, lanes]
        if r == 8:
            return above[f, span, lanes]
        return inner[f, r - 1, span, lanes]

    return load


def groups(members, body):
    def step(g, carry):
        body(pl.multiple_of(g, 1) if False else g)
        return carry

    lax.fori_loop(0, members // 8, step, 0)


def inner_body(state, south, north, inner, west_out, east_out, sems):
    copies = []
    for f in range(3):
        for r in range(1, 7):
            copies.append(
                pltpu.make_async_copy(state.at[:, f, r, :], inner.at[f, r - 1], sems.at[len(copies)])
            )
    for c in copies:
        c.start()
    for c in copies:
        c.wait()
    load = row_loader(inner, south, north)
    groups(state.shape[0], lambda g: put_columns(load, range(8), g, west_out, east_out, None))


def step_row(load, g, r, west, east, push, twof, store):
    lane = lax.broadcasted_iota(jnp.int32, (8, 128), 1)
    first, last = lane == 0, lane == 127
    mid = [[load(f, r, g, c) for c in range(4)] for f in range(3)]
    e, w = [], []
    for f in range(3):
        at = 8 * f + r
        left = [pltpu.roll(x, 127, 1) for x in mid[f]] + [pltpu.roll(east, (127 - at) % 128, 1)]
        right = [pltpu.roll(west, (128 - at) % 128, 1)] + [pltpu.roll(x, 1, 1) for x in mid[f]]
        e.append([jnp.where(last, left[c + 1], left[c]) for c in range(4)])
        w.append([jnp.where(first, right[c], right[c + 1]) for c in range(4)])
    for c in range(4):
        h, u, v = mid[0][c], mid[1][c], mid[2][c]
        he, ue, ve = e[0][c], e[1][c], e[2][c]
        hw, uw, vw = w[0][c], w[1][c], w[2][c]
        hn, un, vn = (load(f, r + 1, g, c) for f in range(3))
        hs, us, vs = (load(f, r - 1, g, c) for f in range(3))
        flux = (he - (he * ue + ue)) + (hw + (hw * uw + uw)) + (hn - (hn * vn + vn)) + (hs + (hs * vs + vs))
        new_h = 0.6 * h + 0.1 * flux + push(r, g, c)
        tu = ((ue + uw) + (un + us)) - (he - hw) - u * (ue - uw) - v * ((un - us) - twof)
        new_u = 0.6 * u + 0.1 * tu
        tv = ((ve + vw) + (vn + vs)) - (hn - hs) - u * ((ve - vw) + twof) - v * (vn - vs)
        new_v = 0.6 * v + 0.1 * tv
        store(r, g, c, (new_h, new_u, new_v))


def push_loader(push):
    return lambda r, g, c: push[r, pl.ds(g * 8, 8), pl.ds(c * 128, 128)]


def step_inner_body(twof, south, inner, north, west, east, push, out):
    load = row_loader(inner, south, north)

    def store(r, g, c, new):
        for f in range(3):
            out[f, r - 1, pl.ds(g * 8, 8), pl.ds(c * 128, 128)] = new[f]

    def body(g):
        wv, ev = west[pl.ds(g * 8, 8), :], east[pl.ds(g * 8, 8), :]
        for r in range(1, 7):
            step_row(load, g, r, wv, ev, push_loader(push), twof[r], store)

    groups(inner.shape[2], body)


def step_outer_body(
    twof, south, inner, north, below, above, west, east, push, fresh, new_south, new_north, west_out, east_out
):
    load = row_loader(inner, south, north, below, above)
    fresh_load = row_loader(fresh, new_south, new_north)

    def store(r, g, c, new):
        out = new_south if r == 0 else new_north
        for f in range(3):
            out[f, pl.ds(g * 8, 8), pl.ds(c * 128, 128)] = new[f]

    def body(g):
        wv, ev = west[pl.ds(g * 8, 8), :], east[pl.ds(g * 8, 8), :]
        for r in (0, 7):
            step_row(load, g, r, wv, ev, push_loader(push), twof[r], store)
        put_columns(fresh_load, range(8), g, west_out, east_out, None)

    groups(inner.shape[2], body)


def push_body(drive, out, sems):
    copies = [pltpu.make_async_copy(drive.at[:, r, :], out.at[r], sems.at[r]) for r in range(8)]
    for c in copies:
        c.start()
    for c in copies:
        c.wait()


def split(x):
    high = x.astype(BF16)
    return high, (x - high.astype(F32)).astype(BF16)


def observe_body(
    twof, south, inner, north, below, above, west, east, push, fresh, index, value, error, new_south, new_north, sums
):
    load = row_loader(inner, south, north, below, above)

    def store(r, g, c, new):
        out = new_south if r == 0 else new_north
        for f in range(3):
            out[f, pl.ds(g * 8, 8), pl.ds(c * 128, 128)] = new[f]

    def body(g):
        wv, ev = west[pl.ds(g * 8, 8), :], east[pl.ds(g * 8, 8), :]
        for r in (0, 7):
            step_row(load, g, r, wv, ev, push_loader(push), twof[r], store)

    groups(inner.shape[2], body)
    obs = index.shape[0]
    lanes = lax.broadcasted_iota(jnp.int32, (obs, 512), 1)
    where_at = jnp.broadcast_to(index[...], (obs, 512))
    seen = jnp.zeros((inner.shape[2], obs), F32)
    for r in range(8):
        pick = jnp.where(where_at == lanes + 512 * r, 1.0, 0.0).astype(BF16)
        height = new_south[0] if r == 0 else new_north[0] if r == 7 else fresh[0, r - 1]
        for part in split(height):
            seen += lax.dot_general(part, pick, (((1,), (1,)), ((), ())), preferred_element_type=F32)
    gram_sums(seen, value, error, sums)


def gram_sums(seen, value, error, sums):
    obs_mean = jnp.mean(seen, axis=0, keepdims=True)
    spread = seen - obs_mean
    inv = 1.0 / error[...]
    pull = inv * (value[...] - obs_mean)
    nt = (((1,), (1,)), ((), ()))
    members = seen.shape[0]
    sums[:members, :] = lax.dot_general(spread * inv, spread, nt, precision=PRECISE, preferred_element_type=F32)
    sums[members:, :] = lax.dot_general(
        jnp.broadcast_to(pull, (8, seen.shape[1])), spread, nt, precision=PRECISE, preferred_element_type=F32
    )


def eye(n):
    return (lax.broadcasted_iota(jnp.int32, (n, n), 0) == lax.broadcasted_iota(jnp.int32, (n, n), 1)).astype(F32)


def split3(x):
    first = x.astype(BF16)
    x = x - first.astype(F32)
    second = x.astype(BF16)
    return first, second, (x - second.astype(F32)).astype(BF16)


def mm(a, b):
    a1, a2, a3 = split3(a)
    b1, b2, b3 = split3(b)
    out = None
    for left, right in (((a1, a3), (b3, b1)), ((a1, a2), (b2, b2)), ((a1, a2), (b1, b1))):
        part = jnp.dot(
            jnp.concatenate(left, axis=1), jnp.concatenate(right, axis=0), preferred_element_type=F32
        )
        out = part if out is None else out + part
    return out


def weights_t(gram, pull):
    n = gram.shape[0]
    ident = eye(n)
    amat = (n - 1) * ident + gram
    scale = jnp.sqrt(jnp.sum(amat * amat, keepdims=True))

    def iterate(_, yz):
        y, z = yz
        p = 1.5 * ident - 0.5 * mm(z, y)
        return mm(y, p), mm(p, z)

    _, z = lax.fori_loop(0, NS_ITERS, iterate, (amat / scale, ident))
    root = z / jnp.sqrt(scale)
    shift = mm(mm(jnp.broadcast_to(pull[0:1], (16, n)), root), root)
    w = math.sqrt(n - 1) * root + shift[0:1, :]
    return w + (1.0 - jnp.sum(w, axis=1, keepdims=True)) / n


def analysis_body(sums, south, inner, north, out, buf, sems):
    n = sums.shape[1]
    w = weights_t(sums[:n, :], sums[n:, :])
    wh, wl = split(w)
    left = [jnp.concatenate([x, x], axis=1) for x in (wh, wl)]
    copies = []
    for r in range(8):
        for f in range(3):
            x = south[f] if r == 0 else north[f] if r == 7 else inner[f, r - 1]
            right = jnp.concatenate(split(x), axis=0)
            buf[f, r] = jnp.dot(left[0], right, preferred_element_type=F32) + jnp.dot(
                left[1], right, preferred_element_type=F32
            )
            c = pltpu.make_async_copy(buf.at[f, r], out.at[:, f, r, :], sems.at[8 * f + r])
            c.start()
            copies.append(c)
    for c in copies:
        c.wait()


def ring(count):
    return [(i, (i + 1) % count) for i in range(count)], [((i + 1) % count, i) for i in range(count)]


def chain(count):
    return [(i, i + 1) for i in range(count - 1)], [(i + 1, i) for i in range(count - 1)]


def swap_rows(south, north):
    up, down = chain(lax.axis_size("lat"))
    return lax.ppermute(north, "lat", up), lax.ppermute(south, "lat", down)


def swap_columns(west, east):
    up, down = ring(lax.axis_size("lon"))
    return lax.ppermute(east, "lon", up), lax.ppermute(west, "lon", down)


def total(x):
    for f in (lambda i: i ^ 1, lambda i: ((i // 2) ^ 1) * 2 + i % 2, lambda i: (3 - i // 2) * 2 + i % 2):
        x = x + lax.ppermute(x, "lon", [(i, f(i)) for i in range(8)])
    for f in (
        lambda i: ((i // 4) ^ 1) * 4 + i % 4,
        lambda i: (3 - i // 4) * 4 + i % 4,
        lambda i: i ^ 1,
        lambda i: (i // 4) * 4 + 3 - i % 4,
    ):
        x = x + lax.ppermute(x, "lat", [(i, f(i)) for i in range(16)])
    return x


def shards(state, drive, obs_index, obs_value, obs_error):
    m, _, rows, cols = state.shape
    obs = obs_index.size
    fill = -obs % 128
    inner_shape, edge, colshape = shape(3, rows - 2, m, cols), shape(3, m, cols), shape(m, 128)
    row = lax.axis_index("lat") * rows + jnp.arange(rows)
    twof = 2.0 * CORIOLIS_MAX * (2.0 * (row.astype(F32) + 0.5) / (rows * lax.axis_size("lat")) - 1.0)

    south, north = call(edge_body, "edges", (edge, edge), [ANY], (VMEM, VMEM), [pltpu.SemaphoreType.DMA((24,))])(state)
    below, above = swap_rows(south, north)
    inner, west, east = call(
        inner_body, "relayout", (inner_shape, colshape, colshape), [ANY, VMEM, VMEM], (VMEM,) * 3,
        [pltpu.SemaphoreType.DMA((18,))],
    )(state, south, north)
    west, east = swap_columns(west, east)
    push = call(push_body, "pushes", shape(rows, m, cols), [ANY], VMEM, [pltpu.SemaphoreType.DMA((8,))])(
        0.5 * drive.astype(F32)
    )
    step_inner = call(step_inner_body, "step_inner", inner_shape, [SMEM] + [VMEM] * 6, VMEM)
    fresh = step_inner(twof, south, inner, north, west, east, push)
    south1, north1, west1, east1 = call(
        step_outer_body, "step_outer", (edge, edge, colshape, colshape), [SMEM] + [VMEM] * 9, (VMEM,) * 4
    )(twof, south, inner, north, below, above, west, east, push, fresh)
    below1, above1 = swap_rows(south1, north1)
    west1, east1 = swap_columns(west1, east1)
    inner2 = step_inner(twof, south1, fresh, north1, west1, east1, push)
    south2, north2, sums = call(
        observe_body, "observe", (edge, edge, shape(m + 8, m)), [SMEM] + [VMEM] * 12, (VMEM,) * 3
    )(
        twof, south1, fresh, north1, below1, above1, west1, east1, push, inner2,
        jnp.pad(obs_index.reshape(obs, 1), ((0, fill), (0, 0)), constant_values=-1),
        jnp.pad(obs_value.reshape(1, obs), ((0, 0), (0, fill))),
        jnp.pad(obs_error.reshape(1, obs), ((0, 0), (0, fill)), constant_values=1.0),
    )
    sums = total(sums)
    return call(
        analysis_body, "analysis", shape(m, 3, rows, cols), [VMEM] * 4, ANY,
        [pltpu.VMEM((3, rows, m, cols), F32), pltpu.SemaphoreType.DMA((24,))],
    )(sums, south2, inner2, north2)


def solution(mesh):
    return jax.shard_map(
        shards,
        mesh=mesh,
        in_specs=(
            P(None, None, "lat", "lon"),
            P(None, "lat", "lon"),
            P("lat", "lon", None),
            P("lat", "lon", None),
            P("lat", "lon", None),
        ),
        out_specs=P(None, None, "lat", "lon"),
        check_vma=False,
    )
```

```python
import functools
import math

import jax
import jax.numpy as jnp
from jax import lax
from jax.experimental import pallas as pl
from jax.experimental.pallas import tpu as pltpu
from jax.sharding import PartitionSpec as P

NS_ITERS = 14
PRECISE = lax.Precision.HIGHEST
CORIOLIS_MAX = 0.3
F32 = jnp.float32
BF16 = jnp.bfloat16

VMEM = pl.BlockSpec(memory_space=pltpu.VMEM)
SMEM = pl.BlockSpec(memory_space=pltpu.SMEM)
HBM = pl.BlockSpec(memory_space=pltpu.HBM)
ANY = pl.BlockSpec(memory_space=pl.ANY)


PLAIN = pl.BlockSpec(memory_space=pltpu.VMEM)


def shape(*dims, dtype=F32):
    return jax.ShapeDtypeStruct(dims, dtype)


def keep(s, spec):
    space = pltpu.VMEM if spec is VMEM else pltpu.HBM if spec is HBM else None
    return s if space is None else space(s.shape, s.dtype)


def call(body, name, outs, ins, out_specs, scratch=(), limit=8, **extra):
    outs = tuple(map(keep, outs, out_specs)) if isinstance(outs, tuple) else keep(outs, out_specs)
    made = pl.pallas_call(
        body,
        name=name,
        out_shape=outs,
        in_specs=ins,
        out_specs=out_specs,
        scratch_shapes=scratch,
        compiler_params=pltpu.CompilerParams(vmem_limit_bytes=limit * 1024 * 1024),
        **extra,
    )

    def run(*args):
        spaces = [pltpu.VMEM if k is VMEM else pltpu.HBM if k is HBM else None for k in ins]
        return made(*(a if k is None else pltpu.with_memory_space_constraint(a, k) for a, k in zip(args, spaces)))

    return run


def odd_row():
    return lax.rem(lax.axis_index("lat"), 2)


def edge_body(state, far, near, sems):
    members = state.shape[0]
    last = state.shape[2] - 1
    parts = 4
    step = members // parts

    def copy(pairs):
        copies = []
        for row, out in pairs:
            for f in range(3):
                for p in range(parts):
                    span = pl.ds(p * step, step)
                    copies.append(
                        pltpu.make_async_copy(state.at[span, f, row, :], out.at[f, span, :], sems.at[len(copies)])
                    )
        for c in copies:
            c.start()
        for c in copies:
            c.wait()

    @pl.when(odd_row() == 0)
    def _():
        copy(((0, far), (last, near)))

    @pl.when(odd_row() == 1)
    def _():
        copy(((last, far), (0, near)))


def put_columns(load, rows, g, outs, start=None):
    lane = lax.broadcasted_iota(jnp.int32, (8, 128), 1)
    span = pl.ds(g * 8, 8)
    west, east = (jnp.zeros((8, 128), F32),) * 2 if start is None else (s[span, :] for s in start)
    for f in range(3):
        for r in rows:
            at = 8 * f + r
            west = jnp.where(lane == at, pltpu.roll(load(f, r, g, 0), at, 1), west)
            east = jnp.where(lane == at, pltpu.roll(load(f, r, g, 3), (at + 1) % 128, 1), east)
    outs[0][span, :] = west
    outs[1][span, :] = east


def row_loader(inner, south, north):
    def load(f, r, g, c):
        span, lanes = pl.ds(g * 8, 8), pl.ds(c * 128, 128)
        if r in (-1, 8):
            return jnp.zeros((8, 128), F32)
        if south is None:
            return inner[f, r, span, lanes]
        if r == 0:
            return south[f, span, lanes]
        if r == 7:
            return north[f, span, lanes]
        return inner[f, r - 1, span, lanes]

    return load


def groups(members, body, unroll=1):
    def step(i, carry):
        for j in range(unroll):
            body(i * unroll + j)
        return carry

    lax.fori_loop(0, members // 8 // unroll, step, 0)


def columns_body(state, west, east, first, last, sems):
    copies = []
    for f in range(3):
        for r in range(8):
            for out, at in ((first, 0), (last, state.shape[3] - 128)):
                copies.append(
                    pltpu.make_async_copy(state.at[:, f, r, pl.ds(at, 128)], out.at[f, r], sems.at[len(copies)])
                )
    for c in copies:
        c.start()
    for c in copies:
        c.wait()

    def load(f, r, g, c):
        return (first if c == 0 else last)[f, r, pl.ds(g * 8, 8), :]

    groups(state.shape[0], lambda g: put_columns(load, range(8), g, (west, east)), 4)


def push_body(drive, push, narrow, wide, sems):
    members, blocks = drive.shape[0], 4
    size = members // blocks
    spans = [pl.ds(b * size, size) for b in range(blocks)]
    loads = [pltpu.make_async_copy(drive.at[s], narrow.at[s], sems.at[b, 8]) for b, s in enumerate(spans)]
    for c in loads:
        c.start()
    copies = []
    for b, span in enumerate(spans):
        loads[b].wait()
        for g in range(b * size // 8, (b + 1) * size // 8):
            wide[pl.ds(g * 8, 8)] = 0.5 * narrow[pl.ds(g * 8, 8)].astype(F32)
        for r in range(8):
            copies.append(pltpu.make_async_copy(wide.at[span, r, :], push.at[r, span, :], sems.at[b, r]))
            copies[-1].start()
    for c in copies:
        c.wait()


def step_row(load, g, r, west, east, push, twof, store):
    lane = lax.broadcasted_iota(jnp.int32, (8, 128), 1)
    first, last = lane == 0, lane == 127
    mid = [[load(f, r, g, c) for c in range(4)] for f in range(3)]
    e, w = [], []
    for f in range(3):
        at = 8 * f + r
        left = [pltpu.roll(x, 127, 1) for x in mid[f]] + [pltpu.roll(east, (127 - at) % 128, 1)]
        right = [pltpu.roll(west, (128 - at) % 128, 1)] + [pltpu.roll(x, 1, 1) for x in mid[f]]
        e.append([jnp.where(last, left[c + 1], left[c]) for c in range(4)])
        w.append([jnp.where(first, right[c], right[c + 1]) for c in range(4)])
    for c in range(4):
        h, u, v = mid[0][c], mid[1][c], mid[2][c]
        he, ue, ve = e[0][c], e[1][c], e[2][c]
        hw, uw, vw = w[0][c], w[1][c], w[2][c]
        hn, un, vn = (load(f, r + 1, g, c) for f in range(3))
        hs, us, vs = (load(f, r - 1, g, c) for f in range(3))
        flux = (he - (he * ue + ue)) + (hw + (hw * uw + uw)) + (hn - (hn * vn + vn)) + (hs + (hs * vs + vs))
        new_h = 0.6 * h + 0.1 * flux + push(r, g, c)
        tu = ((ue + uw) + (un + us)) - (he - hw) - u * (ue - uw) - v * ((un - us) - twof)
        new_u = 0.6 * u + 0.1 * tu
        tv = ((ve + vw) + (vn + vs)) - (hn - hs) - u * ((ve - vw) + twof) - v * (vn - vs)
        new_v = 0.6 * v + 0.1 * tv
        store(r, g, c, (new_h, new_u, new_v))


def step_group(g, twof, load, new_load, west, east, push, new_south, new_inner, new_north, columns=()):
    def take(r, g, c):
        return push[r, pl.ds(g * 8, 8), pl.ds(c * 128, 128)]

    def store(r, g, c, new):
        span, lanes = pl.ds(g * 8, 8), pl.ds(c * 128, 128)
        for f in range(3):
            if r == 0:
                new_south[f, span, lanes] = new[f]
            elif r == 7:
                new_north[f, span, lanes] = new[f]
            else:
                new_inner[f, r - 1, span, lanes] = new[f]

    wv, ev = west[pl.ds(g * 8, 8), :], east[pl.ds(g * 8, 8), :]
    for r in range(8):
        step_row(load, g, r, wv, ev, take, twof[r], store)
    if columns:
        put_columns(new_load, range(1, 7), g, columns)


def first_body(
    twof, state, west, east, push, new_south, new_inner, new_north, new_west, new_east, cells, sems
):
    members, blocks = state.shape[0], 4
    size = members // blocks
    waits = []
    for b in range(blocks):
        span = pl.ds(b * size, size)
        waits.append([])
        for f in range(3):
            for r in range(8):
                waits[b].append(
                    pltpu.make_async_copy(state.at[span, f, r, :], cells.at[f, r, span, :], sems.at[b, len(waits[b])])
                )
                waits[b][-1].start()
    load, new_load = row_loader(cells, None, None), row_loader(new_inner, new_south, new_north)
    for b in range(blocks):
        for c in waits[b]:
            c.wait()

        def step(g, carry):
            step_group(
                g, twof, load, new_load, west, east, push, new_south, new_inner, new_north, (new_west, new_east)
            )
            return carry

        lax.fori_loop(b * size // 8, (b + 1) * size // 8, step, 0)


def second_body(twof, south, inner, north, west, east, push, index, out, new_south, new_north, seen, new, sems):
    load = row_loader(inner, south, north)
    members, blocks = inner.shape[2], 4
    size = members // blocks
    copies = []
    for b in range(blocks):

        def step(g, carry):
            step_group(g, twof, load, None, west, east, push, new_south, new, new_north)
            return carry

        lax.fori_loop(b * size // 8, (b + 1) * size // 8, step, 0)
        span = pl.ds(b * size, size)
        copies.append(pltpu.make_async_copy(new.at[:, :, span, :], out.at[:, :, span, :], sems.at[b]))
        copies[b].start()
    seen[...] = readings(index, [(r, new[0, r - 1]) for r in range(1, 7)])
    for c in copies:
        c.wait()


def outer_row(beyond, centre, part, sign):
    h, u, v = beyond
    at = sign * centre
    return (
        part[0] + 0.1 * (h + sign * (h * v + v)),
        part[1] + 0.1 * (u + at * u),
        part[2] + 0.1 * (v + sign * h + at * v),
    )


def outer_rows(g, centres, beyonds, parts, news):
    span = pl.ds(g * 8, 8)
    for k, sign in ((0, 1.0), (1, -1.0)):
        for c in range(4):
            at = (span, pl.ds(c * 128, 128))
            fresh = outer_row(
                [beyonds[(k, f, *at)] for f in range(3)],
                centres[k][at],
                [parts[k][(f, *at)] for f in range(3)],
                sign,
            )
            for f in range(3):
                news[k][(f, *at)] = fresh[f]


def fetch(far, near, beyonds, sems, blocks=4):
    odd, size = odd_row(), far.shape[1] // blocks
    copies = []
    for b in range(blocks):
        span = pl.ds(b * size, size)
        copies.append(
            [
                pltpu.make_async_copy(far.at[:, span], beyonds.at[odd, :, span], sems.at[b, 0]),
                pltpu.make_async_copy(near.at[:, span], beyonds.at[1 - odd, :, span], sems.at[b, 1]),
            ]
        )
        for c in copies[b]:
            c.start()
    return copies


def outer_body(
    state, far, near, south, north, west, east, new_south, new_north, new_far, new_near, new_west, new_east,
    beyonds, centres, sems, more_sems,
):
    more = [
        pltpu.make_async_copy(state.at[:, 2, row, :], centres.at[k], more_sems.at[k])
        for k, row in enumerate((0, state.shape[2] - 1))
    ]
    for c in more:
        c.start()
    copies = fetch(far, near, beyonds, sems)
    for c in more:
        c.wait()
    load = row_loader(None, new_south, new_north)
    for b, block in enumerate(copies):
        for c in block:
            c.wait()
        for g in range(b * 4, b * 4 + 4):
            outer_rows(g, (centres.at[0], centres.at[1]), beyonds, (south, north), (new_south, new_north))
            put_columns(load, (0, 7), g, (new_west, new_east), (west, east))

    @pl.when(odd_row() == 0)
    def _():
        new_far[...], new_near[...] = new_south[...], new_north[...]

    @pl.when(odd_row() == 1)
    def _():
        new_far[...], new_near[...] = new_north[...], new_south[...]


def split(x):
    high = x.astype(BF16)
    return high, (x - high.astype(F32)).astype(BF16)


def readings(index, rows):
    obs = index.shape[1]
    column = lax.broadcasted_iota(jnp.int32, (512, obs), 0)
    seen = None
    for r, height in rows:
        pick = jnp.where(jnp.broadcast_to(index[...], (512, obs)) == column + 512 * r, 1.0, 0.0).astype(BF16)
        for part in split(height):
            more = jnp.dot(part, pick, preferred_element_type=F32)
            seen = more if seen is None else seen + more
    return seen


def observe_body(
    old_south, old_north, far, near, south, north, index, value, error, seen, out, sums, beyonds, sems, outer, out_sems
):
    copies, stores = fetch(far, near, beyonds, sems), []
    for b, block in enumerate(copies):
        for c in block:
            c.wait()
        for g in range(b * 4, b * 4 + 4):
            outer_rows(
                g, (old_south.at[2], old_north.at[2]), beyonds, (south, north), (outer.at[0], outer.at[1])
            )
        span = pl.ds(b * 32, 32)
        stores.append(pltpu.make_async_copy(outer.at[:, :, span], out.at[:, :, span], out_sems.at[b]))
        stores[b].start()
    more = readings(index, [(0, outer[0, 0]), (7, outer[1, 0])])
    gram_sums(seen[...] + more, value, error, sums)
    for c in stores:
        c.wait()


def fold_body(parts, sums):
    everything = jnp.sum(parts[...], axis=0)
    for i in range(sums.shape[0]):
        sums[i] = everything


def gram_sums(seen, value, error, sums):
    obs_mean = jnp.mean(seen, axis=0, keepdims=True)
    spread = seen - obs_mean
    inv = 1.0 / error[...]
    pull = inv * (value[...] - obs_mean)
    nt = (((1,), (1,)), ((), ()))
    gram = lax.dot_general(spread * inv, spread, nt, precision=PRECISE, preferred_element_type=F32)
    pulls = lax.dot_general(
        jnp.broadcast_to(pull, (8, seen.shape[1])), spread, nt, precision=PRECISE, preferred_element_type=F32
    )
    pack(gram, pulls, sums)


def pack(gram, pulls, sums):
    n = gram.shape[0]
    half = n // 2
    row = lax.broadcasted_iota(jnp.int32, (half, n), 0)
    lane = lax.broadcasted_iota(jnp.int32, (half, n), 1)
    second = pltpu.roll(gram[half:], half, 1)
    packed = jnp.where(lane < row, second, gram[:half])
    diagonal = jnp.sum(jnp.where(lane == row, second, 0.0), axis=0, keepdims=True)
    tail = lax.broadcasted_iota(jnp.int32, (8, n), 0)
    rest = jnp.where(tail == 0, jnp.broadcast_to(diagonal, (8, n)), pulls)
    for i in range(sums.shape[0]):
        sums[i, :half, :] = packed
        sums[i, half:, :] = rest


def unpack(sums):
    n = sums.shape[1]
    half = n // 2
    row = lax.broadcasted_iota(jnp.int32, (half, n), 0)
    lane = lax.broadcasted_iota(jnp.int32, (half, n), 1)
    packed = sums[:half]
    upper = jnp.where(lane < row, 0.0, packed)
    lower = pltpu.roll(jnp.where(lane < row, packed, 0.0), half, 1)
    one = jnp.concatenate([upper, lower], axis=0)
    diagonal = pltpu.roll(sums[half:], half, 1)[0:1]
    return one + one.T + eye(n) * (diagonal - one), sums[half + 1 : half + 2]


def eye(n):
    return (lax.broadcasted_iota(jnp.int32, (n, n), 0) == lax.broadcasted_iota(jnp.int32, (n, n), 1)).astype(F32)


def split3(x):
    first = x.astype(BF16)
    x = x - first.astype(F32)
    second = x.astype(BF16)
    return first, second, (x - second.astype(F32)).astype(BF16)


def mm(a, b):
    a1, a2, a3 = split3(a)
    b1, b2, b3 = split3(b)
    out = None
    for left, right in (((a1, a3), (b3, b1)), ((a1, a2), (b2, b2)), ((a1, a2), (b1, b1))):
        part = jnp.dot(
            jnp.concatenate(left, axis=1), jnp.concatenate(right, axis=0), preferred_element_type=F32
        )
        out = part if out is None else out + part
    return out


def weights_t(gram, pull):
    n = gram.shape[0]
    ident = eye(n)
    amat = (n - 1) * ident + gram
    scale = jnp.sqrt(jnp.sum(amat * amat, keepdims=True))

    y, z = amat / scale, ident
    for _ in range(NS_ITERS):
        p = 1.5 * ident - 0.5 * mm(z, y)
        y, z = mm(y, p), mm(p, z)
    root = z / jnp.sqrt(scale)
    shift = mm(mm(jnp.broadcast_to(pull, (16, n)), root), root)
    w = math.sqrt(n - 1) * root + shift[0:1, :]
    return w + (1.0 - jnp.sum(w, axis=1, keepdims=True)) / n


def analysis_body(sums, outer, inner, out, outers, inners, buf, sems, out_sems):
    loads = [pltpu.make_async_copy(inner, inners, sems.at[0]), pltpu.make_async_copy(outer, outers, sems.at[1])]
    for c in loads:
        c.start()
    w = weights_t(*unpack(jnp.sum(sums[...], axis=0)))
    left = [jnp.concatenate([x, x], axis=1) for x in split(w)]
    for c in loads:
        c.wait()
    copies = []
    for r in range(8):
        for f in range(3):
            right = jnp.concatenate(split(outers[r // 7, f] if r in (0, 7) else inners[f, r - 1]), axis=0)
            buf[f, r] = sum(jnp.dot(piece, right, preferred_element_type=F32) for piece in left)
        for f in range(3):
            copies.append(pltpu.make_async_copy(buf.at[f, r], out.at[:, f, r, :], out_sems.at[8 * f + r]))
            copies[-1].start()
    for c in copies:
        c.wait()


def ring(count):
    return [(i, (i + 1) % count) for i in range(count)], [((i + 1) % count, i) for i in range(count)]


def swap_rows(far, near):
    count = lax.axis_size("lat")

    def swaps(start):
        pairs = [(i, i + 1) for i in range(start, count - 1, 2)]
        return pairs + [(j, i) for i, j in pairs]

    return lax.ppermute(far, "lat", swaps(1)), lax.ppermute(near, "lat", swaps(0))


def swap_columns(west, east):
    up, down = ring(lax.axis_size("lon"))
    return lax.ppermute(east, "lon", up), lax.ppermute(west, "lon", down)


def total(sums):
    lat = lax.axis_size("lat")
    parts = lax.all_to_all(sums, "lon", 0, 0)
    sums = call(fold_body, "fold", shape(lat, *sums.shape[1:]), [PLAIN], PLAIN)(parts)
    return lax.all_to_all(sums, "lat", 0, 0)


def shards(state, drive, obs_index, obs_value, obs_error):
    m, _, rows, cols = state.shape
    obs = obs_index.size
    inner_shape, edge, column, field = shape(3, rows - 2, m, cols), shape(3, m, cols), shape(m, 128), shape(rows, m, cols)
    row = lax.axis_index("lat") * rows + jnp.arange(rows)
    twof = 2.0 * CORIOLIS_MAX * (2.0 * (row.astype(F32) + 0.5) / (rows * lax.axis_size("lat")) - 1.0)
    index, value, error = (x.reshape(1, obs) for x in (obs_index, obs_value, obs_error))

    far, near = call(edge_body, "edges", (edge, edge), [HBM], (VMEM,) * 2, [pltpu.SemaphoreType.DMA((24,))])(state)
    far, near = swap_rows(far, near)
    west, east = call(
        columns_body, "columns", (column, column), [HBM], (VMEM,) * 2,
        [pltpu.VMEM((3, rows, m, 128), F32)] * 2 + [pltpu.SemaphoreType.DMA((48,))], limit=12,
    )(state)
    west, east = swap_columns(west, east)
    push = call(
        push_body, "pushes", field, [HBM], VMEM,
        [pltpu.VMEM(drive.shape, BF16), pltpu.VMEM(drive.shape, F32), pltpu.SemaphoreType.DMA((4, 9))], limit=10,
    )(drive)
    south1, inner1, north1, west1, east1 = call(
        first_body, "first_step", (edge, inner_shape, edge, column, column), [SMEM, HBM] + [VMEM] * 3, (VMEM,) * 5,
        [pltpu.VMEM((3, rows, m, cols), F32), pltpu.SemaphoreType.DMA((4, 24))], limit=12,
    )(twof, state, west, east, push)
    beyonds = [pltpu.VMEM((2, 3, m, cols), F32), pltpu.SemaphoreType.DMA((4, 2))]
    south1, north1, far, near, west1, east1 = call(
        outer_body, "first_outer", (edge, edge, edge, edge, column, column), [HBM, ANY, ANY] + [VMEM] * 4, (VMEM,) * 6,
        [beyonds[0], pltpu.VMEM((2, m, cols), F32), beyonds[1], pltpu.SemaphoreType.DMA((2,))],
    )(state, far, near, south1, north1, west1, east1)
    far, near = swap_rows(far, near)
    west, east = swap_columns(west1, east1)
    inner2, south2, north2, seen = call(
        second_body, "second_step", (inner_shape, edge, edge, shape(m, obs)), [SMEM] + [VMEM] * 7,
        (HBM, VMEM, VMEM, VMEM), [pltpu.VMEM(inner_shape.shape, F32), pltpu.SemaphoreType.DMA((4,))], limit=10,
    )(twof, south1, inner1, north1, west, east, push, index)
    outer2, sums = call(
        observe_body, "observe", (shape(2, 3, m, cols), shape(lax.axis_size("lon"), m // 2 + 8, m)),
        [VMEM, VMEM, ANY, ANY] + [VMEM] * 6, (HBM, PLAIN),
        beyonds + [pltpu.VMEM((2, 3, m, cols), F32), pltpu.SemaphoreType.DMA((4,))],
    )(south1, north1, far, near, south2, north2, index, value, error, seen)
    return call(
        analysis_body, "analysis", shape(m, 3, rows, cols), [PLAIN, HBM, HBM], HBM,
        [
            pltpu.VMEM((2, 3, m, cols), F32),
            pltpu.VMEM(inner_shape.shape, F32),
            pltpu.VMEM((3, rows, m, cols), F32),
            pltpu.SemaphoreType.DMA((2,)),
            pltpu.SemaphoreType.DMA((24,)),
        ],
        limit=24,
    )(total(sums), outer2, inner2)


def solution(mesh):
    return jax.shard_map(
        shards,
        mesh=mesh,
        in_specs=(
            P(None, None, "lat", "lon"),
            P(None, "lat", "lon"),
            P("lat", "lon", None),
            P("lat", "lon", None),
            P("lat", "lon", None),
        ),
        out_specs=P(None, None, "lat", "lon"),
        check_vma=False,
    )
```

```python
import functools
import math

import jax
import jax.numpy as jnp
from jax import lax
from jax.experimental import pallas as pl
from jax.experimental.pallas import tpu as pltpu
from jax.sharding import PartitionSpec as P

NS_ITERS = 14
PRECISE = lax.Precision.HIGHEST
CORIOLIS_MAX = 0.3
F32 = jnp.float32
BF16 = jnp.bfloat16

VMEM = pl.BlockSpec(memory_space=pltpu.VMEM)
SMEM = pl.BlockSpec(memory_space=pltpu.SMEM)
HBM = pl.BlockSpec(memory_space=pltpu.HBM)
ANY = pl.BlockSpec(memory_space=pl.ANY)


PLAIN = pl.BlockSpec(memory_space=pltpu.VMEM)


def shape(*dims, dtype=F32):
    return jax.ShapeDtypeStruct(dims, dtype)


def keep(s, spec):
    space = pltpu.VMEM if spec is VMEM else pltpu.HBM if spec is HBM else None
    return s if space is None else space(s.shape, s.dtype)


def call(body, name, outs, ins, out_specs, scratch=(), limit=4, **extra):
    outs = tuple(map(keep, outs, out_specs)) if isinstance(outs, tuple) else keep(outs, out_specs)
    made = pl.pallas_call(
        body,
        name=name,
        out_shape=outs,
        in_specs=ins,
        out_specs=out_specs,
        scratch_shapes=scratch,
        compiler_params=pltpu.CompilerParams(vmem_limit_bytes=limit * 1024 * 1024),
        **extra,
    )

    def run(*args):
        spaces = [pltpu.VMEM if k is VMEM else pltpu.HBM if k is HBM else None for k in ins]
        return made(*(a if k is None else pltpu.with_memory_space_constraint(a, k) for a, k in zip(args, spaces)))

    return run


def odd_row():
    return lax.rem(lax.axis_index("lat"), 2)


def edge_body(state, far, near, sems):
    members = state.shape[0]
    last = state.shape[2] - 1
    parts = 4
    step = members // parts

    def copy(pairs):
        copies = []
        for row, out in pairs:
            for f in range(3):
                for p in range(parts):
                    span = pl.ds(p * step, step)
                    copies.append(
                        pltpu.make_async_copy(state.at[span, f, row, :], out.at[f, span, :], sems.at[len(copies)])
                    )
        for c in copies:
            c.start()
        for c in copies:
            c.wait()

    @pl.when(odd_row() == 0)
    def _():
        copy(((0, far), (last, near)))

    @pl.when(odd_row() == 1)
    def _():
        copy(((last, far), (0, near)))


def put_columns(load, rows, g, outs, start=None):
    lane = lax.broadcasted_iota(jnp.int32, (8, 128), 1)
    span = pl.ds(g * 8, 8)
    west, east = (jnp.zeros((8, 128), F32),) * 2 if start is None else (s[span, :] for s in start)
    for f in range(3):
        for r in rows:
            at = 8 * f + r
            west = jnp.where(lane == at, pltpu.roll(load(f, r, g, 0), at, 1), west)
            east = jnp.where(lane == at, pltpu.roll(load(f, r, g, 3), (at + 1) % 128, 1), east)
    outs[0][span, :] = west
    outs[1][span, :] = east


def row_loader(inner, south, north):
    def load(f, r, g, c):
        span, lanes = pl.ds(g * 8, 8), pl.ds(c * 128, 128)
        if r in (-1, 8):
            return jnp.zeros((8, 128), F32)
        if south is None:
            return inner[f, r, span, lanes]
        if r == 0:
            return south[f, span, lanes]
        if r == 7:
            return north[f, span, lanes]
        return inner[f, r - 1, span, lanes]

    return load


def groups(members, body, unroll=1):
    def step(i, carry):
        for j in range(unroll):
            body(i * unroll + j)
        return carry

    lax.fori_loop(0, members // 8 // unroll, step, 0)


def columns_body(state, west, east, first, last, sems):
    copies = []
    for f in range(3):
        for r in range(8):
            for out, at in ((first, 0), (last, state.shape[3] - 128)):
                copies.append(
                    pltpu.make_async_copy(state.at[:, f, r, pl.ds(at, 128)], out.at[f, r], sems.at[len(copies)])
                )
    for c in copies:
        c.start()
    for c in copies:
        c.wait()

    def load(f, r, g, c):
        return (first if c == 0 else last)[f, r, pl.ds(g * 8, 8), :]

    groups(state.shape[0], lambda g: put_columns(load, range(8), g, (west, east)), 4)


def push_body(drive, push, narrow, wide, sems):
    members, blocks = drive.shape[0], 4
    size = members // blocks
    spans = [pl.ds(b * size, size) for b in range(blocks)]
    loads = [pltpu.make_async_copy(drive.at[s], narrow.at[s], sems.at[b, 8]) for b, s in enumerate(spans)]
    for c in loads:
        c.start()
    copies = []
    for b, span in enumerate(spans):
        loads[b].wait()
        for g in range(b * size // 8, (b + 1) * size // 8):
            wide[pl.ds(g * 8, 8)] = 0.5 * narrow[pl.ds(g * 8, 8)].astype(F32)
        for r in range(8):
            copies.append(pltpu.make_async_copy(wide.at[span, r, :], push.at[r, span, :], sems.at[b, r]))
            copies[-1].start()
    for c in copies:
        c.wait()


def step_row(load, g, r, west, east, push, twof, store):
    lane = lax.broadcasted_iota(jnp.int32, (8, 128), 1)
    first, last = lane == 0, lane == 127
    mid = [[load(f, r, g, c) for c in range(4)] for f in range(3)]
    e, w = [], []
    for f in range(3):
        at = 8 * f + r
        left = [pltpu.roll(x, 127, 1) for x in mid[f]] + [pltpu.roll(east, (127 - at) % 128, 1)]
        right = [pltpu.roll(west, (128 - at) % 128, 1)] + [pltpu.roll(x, 1, 1) for x in mid[f]]
        e.append([jnp.where(last, left[c + 1], left[c]) for c in range(4)])
        w.append([jnp.where(first, right[c], right[c + 1]) for c in range(4)])
    for c in range(4):
        h, u, v = mid[0][c], mid[1][c], mid[2][c]
        he, ue, ve = e[0][c], e[1][c], e[2][c]
        hw, uw, vw = w[0][c], w[1][c], w[2][c]
        hn, un, vn = (load(f, r + 1, g, c) for f in range(3))
        hs, us, vs = (load(f, r - 1, g, c) for f in range(3))
        flux = (he - (he * ue + ue)) + (hw + (hw * uw + uw)) + (hn - (hn * vn + vn)) + (hs + (hs * vs + vs))
        new_h = 0.6 * h + 0.1 * flux + push(r, g, c)
        tu = ((ue + uw) + (un + us)) - (he - hw) - u * (ue - uw) - v * ((un - us) - twof)
        new_u = 0.6 * u + 0.1 * tu
        tv = ((ve + vw) + (vn + vs)) - (hn - hs) - u * ((ve - vw) + twof) - v * (vn - vs)
        new_v = 0.6 * v + 0.1 * tv
        store(r, g, c, (new_h, new_u, new_v))


def step_group(g, twof, load, new_load, west, east, push, new_south, new_inner, new_north, columns=()):
    def take(r, g, c):
        return push[r, pl.ds(g * 8, 8), pl.ds(c * 128, 128)]

    def store(r, g, c, new):
        span, lanes = pl.ds(g * 8, 8), pl.ds(c * 128, 128)
        for f in range(3):
            if r == 0:
                new_south[f, span, lanes] = new[f]
            elif r == 7:
                new_north[f, span, lanes] = new[f]
            else:
                new_inner[f, r - 1, span, lanes] = new[f]

    wv, ev = west[pl.ds(g * 8, 8), :], east[pl.ds(g * 8, 8), :]
    for r in range(8):
        step_row(load, g, r, wv, ev, take, twof[r], store)
    if columns:
        put_columns(new_load, range(1, 7), g, columns)


def first_body(
    twof, state, west, east, push, new_south, new_inner, new_north, new_west, new_east, cells, sems
):
    members, blocks = state.shape[0], 4
    size = members // blocks
    waits = []
    for b in range(blocks):
        span = pl.ds(b * size, size)
        waits.append([])
        for f in range(3):
            for r in range(8):
                waits[b].append(
                    pltpu.make_async_copy(state.at[span, f, r, :], cells.at[f, r, span, :], sems.at[b, len(waits[b])])
                )
                waits[b][-1].start()
    load, new_load = row_loader(cells, None, None), row_loader(new_inner, new_south, new_north)
    for b in range(blocks):
        for c in waits[b]:
            c.wait()

        def step(g, carry):
            step_group(
                g, twof, load, new_load, west, east, push, new_south, new_inner, new_north, (new_west, new_east)
            )
            return carry

        lax.fori_loop(b * size // 8, (b + 1) * size // 8, step, 0)


def second_body(twof, south, inner, north, west, east, push, index, out, new_south, new_north, seen, new, sems):
    load = row_loader(inner, south, north)
    members, blocks = inner.shape[2], 4
    size = members // blocks
    copies = []
    for b in range(blocks):

        def step(g, carry):
            step_group(g, twof, load, None, west, east, push, new_south, new, new_north)
            return carry

        lax.fori_loop(b * size // 8, (b + 1) * size // 8, step, 0)
        span = pl.ds(b * size, size)
        copies.append(pltpu.make_async_copy(new.at[:, :, span, :], out.at[:, :, span, :], sems.at[b]))
        copies[b].start()
    seen[...] = readings(index, [(r, new[0, r - 1]) for r in range(1, 7)])
    for c in copies:
        c.wait()


def outer_row(beyond, centre, part, sign):
    h, u, v = beyond
    at = sign * centre
    return (
        part[0] + 0.1 * (h + sign * (h * v + v)),
        part[1] + 0.1 * (u + at * u),
        part[2] + 0.1 * (v + sign * h + at * v),
    )


def outer_rows(g, centres, beyonds, parts, news):
    span = pl.ds(g * 8, 8)
    for k, sign in ((0, 1.0), (1, -1.0)):
        for c in range(4):
            at = (span, pl.ds(c * 128, 128))
            fresh = outer_row(
                [beyonds[(k, f, *at)] for f in range(3)],
                centres[k][at],
                [parts[k][(f, *at)] for f in range(3)],
                sign,
            )
            for f in range(3):
                news[k][(f, *at)] = fresh[f]


def fetch(far, near, beyonds, sems, blocks=4):
    odd, size = odd_row(), far.shape[1] // blocks
    copies = []
    for b in range(blocks):
        span = pl.ds(b * size, size)
        copies.append(
            [
                pltpu.make_async_copy(far.at[:, span], beyonds.at[odd, :, span], sems.at[b, 0]),
                pltpu.make_async_copy(near.at[:, span], beyonds.at[1 - odd, :, span], sems.at[b, 1]),
            ]
        )
        for c in copies[b]:
            c.start()
    return copies


def outer_body(
    state, far, near, south, north, west, east, new_south, new_north, new_far, new_near, new_west, new_east,
    beyonds, centres, sems, more_sems,
):
    more = [
        pltpu.make_async_copy(state.at[:, 2, row, :], centres.at[k], more_sems.at[k])
        for k, row in enumerate((0, state.shape[2] - 1))
    ]
    for c in more:
        c.start()
    copies = fetch(far, near, beyonds, sems)
    for c in more:
        c.wait()
    load = row_loader(None, new_south, new_north)
    for b, block in enumerate(copies):
        for c in block:
            c.wait()
        for g in range(b * 4, b * 4 + 4):
            outer_rows(g, (centres.at[0], centres.at[1]), beyonds, (south, north), (new_south, new_north))
            put_columns(load, (0, 7), g, (new_west, new_east), (west, east))

    @pl.when(odd_row() == 0)
    def _():
        new_far[...], new_near[...] = new_south[...], new_north[...]

    @pl.when(odd_row() == 1)
    def _():
        new_far[...], new_near[...] = new_north[...], new_south[...]


def split(x):
    high = x.astype(BF16)
    return high, (x - high.astype(F32)).astype(BF16)


def readings(index, rows):
    obs = index.shape[1]
    column = lax.broadcasted_iota(jnp.int32, (512, obs), 0)
    seen = None
    for r, height in rows:
        pick = jnp.where(jnp.broadcast_to(index[...], (512, obs)) == column + 512 * r, 1.0, 0.0).astype(BF16)
        for part in split(height):
            more = jnp.dot(part, pick, preferred_element_type=F32)
            seen = more if seen is None else seen + more
    return seen


def observe_body(far, near, south, north, index, value, error, seen, sums, beyonds, sems):
    copies = []
    for k, source in ((odd_row(), far), (1 - odd_row(), near)):
        for i, f in enumerate((0, 2)):
            copies.append(pltpu.make_async_copy(source.at[f], beyonds.at[k, i], sems.at[len(copies)]))
            copies[-1].start()
    for c in copies:
        c.wait()
    rows = []
    for k, (r, part, sign) in enumerate(((0, south, 1.0), (7, north, -1.0))):
        h, v = beyonds[k, 0], beyonds[k, 1]
        rows.append((r, part[0] + 0.1 * (h + sign * (h * v + v))))
    gram_sums(seen[...] + readings(index, rows), value, error, sums)


def gram_sums(seen, value, error, sums):
    obs_mean = jnp.mean(seen, axis=0, keepdims=True)
    spread = seen - obs_mean
    inv = 1.0 / error[...]
    pull = inv * (value[...] - obs_mean)
    nt = (((1,), (1,)), ((), ()))
    gram = lax.dot_general(spread * inv, spread, nt, precision=PRECISE, preferred_element_type=F32)
    pulls = lax.dot_general(
        jnp.broadcast_to(pull, (8, seen.shape[1])), spread, nt, precision=PRECISE, preferred_element_type=F32
    )
    pack(gram, pulls, sums)


def pack(gram, pulls, sums):
    n = gram.shape[0]
    half = n // 2
    row = lax.broadcasted_iota(jnp.int32, (half, n), 0)
    lane = lax.broadcasted_iota(jnp.int32, (half, n), 1)
    second = pltpu.roll(gram[half:], half, 1)
    packed = jnp.where(lane < row, second, gram[:half])
    diagonal = jnp.sum(jnp.where(lane == row, second, 0.0), axis=0, keepdims=True)
    tail = lax.broadcasted_iota(jnp.int32, (8, n), 0)
    rest = jnp.where(tail == 0, jnp.broadcast_to(diagonal, (8, n)), pulls)
    sums[:half, :] = packed
    sums[half:, :] = rest


def unpack(sums):
    n = sums.shape[1]
    half = n // 2
    row = lax.broadcasted_iota(jnp.int32, (half, n), 0)
    lane = lax.broadcasted_iota(jnp.int32, (half, n), 1)
    packed = sums[:half]
    upper = jnp.where(lane < row, 0.0, packed)
    lower = pltpu.roll(jnp.where(lane < row, packed, 0.0), half, 1)
    one = jnp.concatenate([upper, lower], axis=0)
    diagonal = pltpu.roll(sums[half:], half, 1)[0:1]
    return one + one.T + eye(n) * (diagonal - one), sums[half + 1 : half + 2]


def eye(n):
    return (lax.broadcasted_iota(jnp.int32, (n, n), 0) == lax.broadcasted_iota(jnp.int32, (n, n), 1)).astype(F32)


def split3(x):
    first = x.astype(BF16)
    x = x - first.astype(F32)
    second = x.astype(BF16)
    return first, second, (x - second.astype(F32)).astype(BF16)


def mm(a, b):
    a1, a2, a3 = split3(a)
    b1, b2, b3 = split3(b)
    out = None
    for left, right in (((a1, a3), (b3, b1)), ((a1, a2), (b2, b2)), ((a1, a2), (b1, b1))):
        part = jnp.dot(
            jnp.concatenate(left, axis=1), jnp.concatenate(right, axis=0), preferred_element_type=F32
        )
        out = part if out is None else out + part
    return out


def weights_t(gram, pull):
    n = gram.shape[0]
    ident = eye(n)
    amat = (n - 1) * ident + gram
    scale = jnp.sqrt(jnp.sum(amat * amat, keepdims=True))

    y = amat / scale
    z = 1.5 * ident - 0.5 * y
    y = mm(y, z)

    def iterate(_, yz):
        y, z = yz
        p = 1.5 * ident - 0.5 * mm(z, y)
        return mm(y, p), mm(p, z)

    _, z = lax.fori_loop(0, NS_ITERS - 1, iterate, (y, z))
    root = z / jnp.sqrt(scale)
    shift = mm(mm(jnp.broadcast_to(pull, (16, n)), root), root)
    w = math.sqrt(n - 1) * root + shift[0:1, :]
    return w + (1.0 - jnp.sum(w, axis=1, keepdims=True)) / n


def analysis_body(
    sums, old_south, old_north, far, near, south, north, inner, out, inners, outers, beyonds, centres, buf, sems,
    out_sems,
):
    odd = odd_row()
    loads = [
        pltpu.make_async_copy(a, b, sems.at[i])
        for i, (a, b) in enumerate(
            (
                (inner, inners),
                (south, outers.at[0]),
                (north, outers.at[1]),
                (far, beyonds.at[odd]),
                (near, beyonds.at[1 - odd]),
                (old_south.at[2], centres.at[0]),
                (old_north.at[2], centres.at[1]),
            )
        )
    ]
    for c in loads:
        c.start()
    w = weights_t(*unpack(sums[...]))
    left = [jnp.concatenate([x, x], axis=1) for x in split(w)]
    for c in loads:
        c.wait()
    copies = []
    for r in (1, 2, 3, 4, 5, 6, 0, 7):
        if r in (0, 7):
            k = r // 7
            part = outer_row(
                [beyonds[k, f] for f in range(3)], centres[k], [outers[k, f] for f in range(3)], 1.0 - 2.0 * k
            )
        else:
            part = [inners[f, r - 1] for f in range(3)]
        for f in range(3):
            right = jnp.concatenate(split(part[f]), axis=0)
            buf[f, r] = sum(jnp.dot(piece, right, preferred_element_type=F32) for piece in left)
        for f in range(3):
            copies.append(pltpu.make_async_copy(buf.at[f, r], out.at[:, f, r, :], out_sems.at[8 * f + r]))
            copies[-1].start()
    for c in copies:
        c.wait()


def ring(count):
    return [(i, (i + 1) % count) for i in range(count)], [((i + 1) % count, i) for i in range(count)]


def swap_rows(far, near):
    count = lax.axis_size("lat")

    def swaps(start):
        pairs = [(i, i + 1) for i in range(start, count - 1, 2)]
        return pairs + [(j, i) for i, j in pairs]

    return lax.ppermute(far, "lat", swaps(1)), lax.ppermute(near, "lat", swaps(0))


def swap_columns(west, east):
    up, down = ring(lax.axis_size("lon"))
    return lax.ppermute(east, "lon", up), lax.ppermute(west, "lon", down)


def total(x):
    for axis, bits in (("lon", (1,)), ("lon", (2, 4, 6)), ("lat", (4, 8, 12)), ("lat", (1, 2, 3))):
        count = lax.axis_size(axis)
        parts = [lax.ppermute(x, axis, [(i, i ^ bit) for i in range(count)]) for bit in bits]
        for part in parts:
            x = x + part
    return x


def shards(state, drive, obs_index, obs_value, obs_error):
    m, _, rows, cols = state.shape
    obs = obs_index.size
    inner_shape, edge, column, field = shape(3, rows - 2, m, cols), shape(3, m, cols), shape(m, 128), shape(rows, m, cols)
    row = lax.axis_index("lat") * rows + jnp.arange(rows)
    twof = 2.0 * CORIOLIS_MAX * (2.0 * (row.astype(F32) + 0.5) / (rows * lax.axis_size("lat")) - 1.0)
    index, value, error = (x.reshape(1, obs) for x in (obs_index, obs_value, obs_error))

    far, near = call(edge_body, "edges", (edge, edge), [HBM], (VMEM,) * 2, [pltpu.SemaphoreType.DMA((24,))])(state)
    far, near = swap_rows(far, near)
    west, east = call(
        columns_body, "columns", (column, column), [HBM], (VMEM,) * 2,
        [pltpu.VMEM((3, rows, m, 128), F32)] * 2 + [pltpu.SemaphoreType.DMA((48,))], limit=5,
    )(state)
    west, east = swap_columns(west, east)
    push = call(
        push_body, "pushes", field, [HBM], VMEM,
        [pltpu.VMEM(drive.shape, BF16), pltpu.VMEM(drive.shape, F32), pltpu.SemaphoreType.DMA((4, 9))], limit=5,
    )(drive)
    south1, inner1, north1, west1, east1 = call(
        first_body, "first_step", (edge, inner_shape, edge, column, column), [SMEM, HBM] + [VMEM] * 3, (VMEM,) * 5,
        [pltpu.VMEM((3, rows, m, cols), F32), pltpu.SemaphoreType.DMA((4, 24))], limit=8,
    )(twof, state, west, east, push)
    beyonds = [pltpu.VMEM((2, 3, m, cols), F32), pltpu.SemaphoreType.DMA((4, 2))]
    south1, north1, far, near, west1, east1 = call(
        outer_body, "first_outer", (edge, edge, edge, edge, column, column), [HBM, ANY, ANY] + [VMEM] * 4, (VMEM,) * 6,
        [beyonds[0], pltpu.VMEM((2, m, cols), F32), beyonds[1], pltpu.SemaphoreType.DMA((2,))],
    )(state, far, near, south1, north1, west1, east1)
    far, near = swap_rows(far, near)
    west, east = swap_columns(west1, east1)
    inner2, south2, north2, seen = call(
        second_body, "second_step", (inner_shape, edge, edge, shape(m, obs)), [SMEM] + [VMEM] * 7,
        (HBM, VMEM, VMEM, VMEM), [pltpu.VMEM(inner_shape.shape, F32), pltpu.SemaphoreType.DMA((4,))], limit=7,
    )(twof, south1, inner1, north1, west, east, push, index)
    sums = call(
        observe_body, "observe", shape(m // 2 + 8, m), [ANY, ANY] + [VMEM] * 6, PLAIN,
        [pltpu.VMEM((2, 2, m, cols), F32), pltpu.SemaphoreType.DMA((4,))],
    )(far, near, south2, north2, index, value, error, seen)
    return call(
        analysis_body, "analysis", shape(m, 3, rows, cols), [PLAIN] + [HBM] * 7, HBM,
        [
            pltpu.VMEM(inner_shape.shape, F32),
            pltpu.VMEM((2, 3, m, cols), F32),
            pltpu.VMEM((2, 3, m, cols), F32),
            pltpu.VMEM((2, m, cols), F32),
            pltpu.VMEM((3, rows, m, cols), F32),
            pltpu.SemaphoreType.DMA((7,)),
            pltpu.SemaphoreType.DMA((24,)),
        ],
        limit=24,
    )(total(sums), south1, north1, far, near, south2, north2, inner2)


def solution(mesh):
    return jax.shard_map(
        shards,
        mesh=mesh,
        in_specs=(
            P(None, None, "lat", "lon"),
            P(None, "lat", "lon"),
            P("lat", "lon", None),
            P("lat", "lon", None),
            P("lat", "lon", None),
        ),
        out_specs=P(None, None, "lat", "lon"),
        check_vma=False,
    )
```
